32 devices in a mesh: rows: 8 (over z, y), cols: 4 (over x, core).
Axes of the slice: x: 2, y: 2, z: 4, core: 2. Of those that a mesh axis runs over, the one named last changes fastest.
Arguments:
- right_leaf: float32 [4, 2048, 128], P(None, 'rows'), may hold values from -6 to 6
- right_mid: float32 [2, 4096, 128], P(None, 'rows'), may hold values from -6 to 6
- right_root: float32 [8192, 128], P('rows'), may hold values from -6 to 6
- inverse_leaf: float32 [4, 2048, 2048], P(None, 'rows', 'cols'), may hold values from -1 to 2, as said below
- inverse_mid: float32 [2, 4096, 4096], P(None, 'rows', 'cols'), may hold values from -1 to 2, as said below
- inverse_root: float32 [8192, 8192], P('rows', 'cols'), may hold values from -1 to 2, as said below
- leaf_to_mid: float32 [4, 4096, 2048], P(None, 'rows', 'cols'), may hold values from -0.125 to 0.125
- leaf_to_root: float32 [4, 8192, 2048], P(None, 'rows', 'cols'), may hold values from -0.125 to 0.125
- mid_to_root: float32 [2, 8192, 4096], P(None, 'rows', 'cols'), may hold values from -0.09375 to 0.09375
- mask_leaf_mid: int32 [4, 32, 16], replicated, may hold values 0 or 1
- mask_leaf_root: int32 [4, 64, 16], replicated, may hold values 0 or 1
- mask_mid_root: int32 [2, 64, 32], replicated, may hold values 0 or 1
Outputs:
- solved_leaf: float32 [4, 2048, 128], P(None, 'rows')
- solved_mid: float32 [2, 4096, 128], P(None, 'rows')
- solved_root: float32 [8192, 128], P('rows')
The draws below stay inside these ranges and needn't reach their ends.
Inputs may be any that keep to these rules, and one draw needn't show every extreme that they name: `inverse_leaf`: lower triangular, with its diagonal between 0.5 and 2. `inverse_mid`: lower triangular, with its diagonal between 0.5 and 2. `inverse_root`: lower triangular, with its diagonal between 0.5 and 2.
All inputs are finite; a program needn't handle non-finite values.
Results may differ from the reference program's by a relative error of at most 0.00014.
Values sent between devices are 32-bit elements; how exact they have to be, the bound alone decides.
No kernel may reach another device: no remote copies, remote signals or barrier semaphores. Data moves between devices by JAX's collectives and lax.ppermute only.
A program may use at most 128 MiB of HBM per device.

```python
import jax
import jax.numpy as jnp
from jax import lax

S2 = 2048
S1 = 4096
S0 = 8192
TILE = 128
NRHS = 128


def lower_inverse(key, count, order):
    key_off, key_diag = jax.random.split(key)
    row_ids = jnp.arange(order)[:, None]
    col_ids = jnp.arange(order)[None, :]
    offdiag = jax.random.normal(key_off, (count, order, order), jnp.float32)
    diagonal = jax.random.uniform(key_diag, (count, order, 1), jnp.float32, 0.6, 1.4)
    offdiag = jnp.clip(offdiag, -6.0, 6.0) / jnp.sqrt(jnp.float32(order))
    lower = jnp.where(row_ids > col_ids, offdiag, jnp.float32(0.0))
    return jnp.where(row_ids == col_ids, diagonal, lower).astype(jnp.float32)


def draw_inverse_leaf(key, part):
    return lower_inverse(jax.random.fold_in(key, 11), 4, S2)


def draw_inverse_mid(key, part):
    return lower_inverse(jax.random.fold_in(key, 12), 2, S1)


def draw_inverse_root(key, part):
    return lower_inverse(jax.random.fold_in(key, 13), 1, S0)[0]


def place_ends(entries, key, least, top_value):
    index_at = [jax.random.randint(jax.random.fold_in(key, axis), (), 0, length) for axis, length in enumerate(entries.shape)]
    longest = entries.shape.index(max(entries.shape))
    beside = index_at[:longest] + [(index_at[longest] + 1) % entries.shape[longest]] + index_at[longest + 1:]
    return entries.at[tuple(index_at)].set(least).at[tuple(beside)].set(top_value)


def block_levels(stream_key, extent, cuts, least, largest):
    factor_of, own = 1.0, jax.random.fold_in(stream_key, 6)
    for dim, blocks in cuts:
        heights = jnp.exp(jax.random.uniform(jax.random.fold_in(own, dim), (blocks,), jnp.float32, least / len(cuts), largest / len(cuts)))
        factor_of = factor_of * jnp.repeat(heights, extent[dim] // blocks).reshape([-1 if axis == dim else 1 for axis in range(len(extent))])
    return factor_of


def noise(rng, dims, scale, reach, shards=(), held_as=jnp.bfloat16):
    entries = jax.random.normal(rng, dims, jnp.float32) * scale
    if len(shards) > 0:
        entries = block_levels(rng, dims, shards, -0.22, 0.18) * entries
    return jnp.clip(entries, min=-reach, max=reach).astype(held_as)


def setup_inputs(seed: int = 0) -> dict:
    keys = jax.random.split(jax.random.key(seed), 13)
    return {
        "right_leaf": noise(keys[0], (4, S2, NRHS), 1.0, 6.0, ((1, 8),), jnp.float32),
        "right_mid": noise(keys[1], (2, S1, NRHS), 1.0, 6.0, ((1, 8),), jnp.float32),
        "right_root": noise(keys[2], (S0, NRHS), 1.0, 6.0, ((0, 8),), jnp.float32),
        "inverse_leaf": draw_inverse_leaf(jax.random.fold_in(keys[12], 71), 0),
        "inverse_mid": draw_inverse_mid(jax.random.fold_in(keys[12], 71), 0),
        "inverse_root": draw_inverse_root(jax.random.fold_in(keys[12], 71), 0),
        "leaf_to_mid": noise(keys[6], (4, S1, S2), S2 ** -0.5, 0.125, ((1, 8), (2, 4)), jnp.float32),
        "leaf_to_root": noise(keys[7], (4, S0, S2), S2 ** -0.5, 0.125, ((1, 8), (2, 4)), jnp.float32),
        "mid_to_root": noise(keys[8], (2, S0, S1), S1 ** -0.5, 0.09375, ((1, 8), (2, 4)), jnp.float32),
        "mask_leaf_mid": place_ends((jax.random.randint(keys[9], (4, S1 // TILE, S2 // TILE), 0, 2) < 1).astype(jnp.int32), jax.random.fold_in(keys[9], 1), 0, 1),
        "mask_leaf_root": place_ends((jax.random.randint(keys[10], (4, S0 // TILE, S2 // TILE), 0, 2) < 1).astype(jnp.int32), jax.random.fold_in(keys[10], 1), 0, 1),
        "mask_mid_root": place_ends((jax.random.randint(keys[11], (2, S0 // TILE, S1 // TILE), 0, 2) < 1).astype(jnp.int32), jax.random.fold_in(keys[11], 1), 0, 1),
    }


def expand(pattern):
    return jnp.repeat(jnp.repeat(pattern.astype(jnp.float32), TILE, axis=1), TILE, axis=2)


def apply(matrix, vector):
    return jnp.einsum('src,sck->srk', matrix, vector, precision=lax.Precision.HIGHEST)


def reference(right_leaf, right_mid, right_root, inverse_leaf, inverse_mid, inverse_root, leaf_to_mid, leaf_to_root, mid_to_root, mask_leaf_mid, mask_leaf_root, mask_mid_root):
    solved_leaf = apply(inverse_leaf, right_leaf)
    mid_terms = apply(leaf_to_mid * expand(mask_leaf_mid), solved_leaf)
    resid_mid = right_mid - mid_terms.reshape(2, 2, S1, NRHS).sum(axis=1)
    root_terms = apply(leaf_to_root * expand(mask_leaf_root), solved_leaf).sum(axis=0)
    solved_mid = apply(inverse_mid, resid_mid)
    root_more = apply(mid_to_root * expand(mask_mid_root), solved_mid).sum(axis=0)
    resid_root = right_root - root_terms - root_more
    solved_root = jnp.dot(inverse_root, resid_root, precision=lax.Precision.HIGHEST)
    return solved_leaf, solved_mid, solved_root
```

```python
import functools

import jax
import jax.numpy as jnp
from jax import lax
from jax.experimental import pallas as pl
from jax.experimental.pallas import tpu as pltpu
from jax.sharding import PartitionSpec as P

TILE = 128
AXES = ("rows", "cols")
BF16 = jnp.bfloat16
F32 = jnp.float32


def product(matrix, vector):
    return jnp.einsum(
        "src,sck->srk",
        matrix,
        vector,
        precision=lax.Precision.HIGHEST,
        preferred_element_type=jnp.float32,
    )


def masked(values, pattern):
    rows_dev = values.shape[1]
    cols_dev = values.shape[2]
    row_ids = lax.axis_index("rows") * rows_dev + lax.iota(jnp.int32, rows_dev)
    col_ids = lax.axis_index("cols") * cols_dev + lax.iota(jnp.int32, cols_dev)
    row_hot = (row_ids[:, None] // TILE == lax.iota(jnp.int32, pattern.shape[1])[None, :]).astype(F32)
    col_hot = (col_ids[:, None] // TILE == lax.iota(jnp.int32, pattern.shape[2])[None, :]).astype(F32)
    return values * jnp.einsum("ra,sab,cb->src", row_hot, pattern.astype(F32), col_hot)


def fetch_columns(block):
    gathered = lax.all_gather(block, "rows", axis=1, tiled=True)
    col_width = gathered.shape[1] // lax.axis_size("cols")
    return lax.dynamic_slice_in_dim(gathered, lax.axis_index("cols") * col_width, col_width, 1)


def general_body(
    right_leaf,
    right_mid,
    right_root,
    inverse_leaf,
    inverse_mid,
    inverse_root,
    leaf_to_mid,
    leaf_to_root,
    mid_to_root,
    mask_leaf_mid,
    mask_leaf_root,
    mask_mid_root,
):
    factor_lm = masked(leaf_to_mid, mask_leaf_mid)
    factor_lr = masked(leaf_to_root, mask_leaf_root)
    factor_mr = masked(mid_to_root, mask_mid_root)
    solved_leaf = lax.psum(product(inverse_leaf, fetch_columns(right_leaf)), "cols")
    leaf_columns = fetch_columns(solved_leaf)
    terms = product(factor_lm, leaf_columns)
    mid_part = terms.reshape(2, 2, terms.shape[1], terms.shape[2]).sum(axis=1)
    resid_mid = right_mid - lax.psum(mid_part, "cols")
    solved_mid = lax.psum(product(inverse_mid, fetch_columns(resid_mid)), "cols")
    mid_columns = fetch_columns(solved_mid)
    root_part = product(factor_lr, leaf_columns).sum(axis=0) + product(factor_mr, mid_columns).sum(axis=0)
    resid_root = right_root - lax.psum(root_part, "cols")
    solved_root = lax.psum(product(inverse_root[None], fetch_columns(resid_root[None])), "cols")
    return (solved_leaf, solved_mid, solved_root[0])


PIECE = 256


def flat(x, y, z, k):
    return (2 * z + y) * 4 + 2 * x + k


PLACES = [(x, y, z, k) for x in (0, 1) for y in (0, 1) for z in range(4) for k in (0, 1)]
TO_CORE = [(flat(x, y, z, k), flat(x, y, z, 1 - k)) for x, y, z, k in PLACES]
TO_X = [(flat(x, y, z, k), flat(1 - x, y, z, k)) for x, y, z, k in PLACES]
TO_Y = [(flat(x, y, z, k), flat(x, 1 - y, z, k)) for x, y, z, k in PLACES]
TO_Z = [(flat(x, y, z, k), flat(x, y, z ^ 1, k)) for x, y, z, k in PLACES]
TO_YZ = [(flat(x, y, z, k), flat(x, 1 - y, z ^ 1, k)) for x, y, z, k in PLACES]
TO_FAR = [(flat(x, y, z, k), flat(x, y, z ^ 2, k)) for x, y, z, k in PLACES if z // 2 == x]


def send(value, pairs):
    return lax.ppermute(value, AXES, pairs)


def place():
    r, c = lax.axis_index("rows"), lax.axis_index("cols")
    return c // 2, r % 2, r // 2, c % 2


def halve(part):
    k = place()[3]
    other = send(part, TO_CORE)
    mine = lax.dynamic_index_in_dim(part, k, 0, False) + lax.dynamic_index_in_dim(other, k, 0, False)
    return mine, send(mine, TO_X)


def both_halves(mine):
    k = place()[3]
    other = send(mine, TO_CORE)
    first = k == 0
    return jnp.stack([jnp.where(first, mine, other), jnp.where(first, other, mine)])


def spread(mine):
    x, y, z, k = place()
    far = send(mine, TO_FAR)
    own = jnp.where(z // 2 == x, mine, far)
    beside, above, across = send(own, TO_Y), send(own, TO_Z), send(own, TO_YZ)
    same = (z % 2) == k
    swapped = send(jnp.stack([jnp.where(same, above, own), jnp.where(same, across, beside)]), TO_CORE)
    return own, beside, above, across, swapped


def split(value):
    high = value.astype(BF16)
    return high, (value - high.astype(F32)).astype(BF16)


def kernel_body(spans, has_mask, has_add, separate, leafwise, *refs):
    own, beside, above, across, swapped = refs[:5]
    refs = refs[5:]
    count = len(spans)
    mats, refs = refs[:count], refs[count:]
    if has_mask:
        mask, refs = refs[0], refs[1:]
    if has_add:
        add, refs = refs[0], refs[1:]
    out, held = refs
    step = pl.program_id(0)
    n = out.shape[-1]

    @pl.when(step == 0)
    def _():
        r, c = lax.axis_index("rows"), lax.axis_index("cols")
        y, k = lax.rem(r, 2), lax.rem(c, 2)
        same = lax.rem(r // 2, 2) == k

        def put(value, y_of, half):
            row = half * (2 * PIECE) + y_of * PIECE if leafwise else y_of * (2 * PIECE) + half * PIECE
            row = pl.multiple_of(row, PIECE)
            high, low = split(value)
            held[pl.ds(row, PIECE), :n] = high
            held[pl.ds(row, PIECE), n:] = low

        @pl.when(same)
        def _():
            put(own[...], y, k)
            put(beside[...], 1 - y, k)

        @pl.when(jnp.logical_not(same))
        def _():
            put(above[...], y, k)
            put(across[...], 1 - y, k)

        put(swapped[0], y, 1 - k)
        put(swapped[1], 1 - y, 1 - k)

    total = None
    for t, (start, width) in enumerate(spans):
        leaf = t if len(mats) == 1 or mats[t].ndim == 3 else 0
        a = mats[t][0] if mats[t].ndim == 3 else mats[t][...]
        if has_mask:
            rows = a.shape[0] // TILE
            a = jnp.concatenate(
                [a[q * TILE : (q + 1) * TILE] * mask[t, pl.ds(step * rows + q, 1), :] for q in range(rows)], axis=0
            )
        high, low = split(a)
        x = held[start : start + width, :]
        wide = jnp.dot(high, x, preferred_element_type=F32)
        value = jnp.dot(low, x[:, :n], preferred_element_type=F32) + wide[:, n:] + wide[:, :n]
        if separate:
            out[t] = value
        else:
            total = value if total is None else total + value
    if not separate:
        if has_add:
            total = total + add[...]
        out[...] = total


def apply(pieces, terms, rows, row_tile, first_tile=0, mask=None, add=None, separate=False, leafwise=False):
    n = pieces[0].shape[-1]
    steps = rows // row_tile
    full = lambda a: pl.BlockSpec(a.shape, lambda i, d=a.ndim: (0,) * d)
    operands = list(pieces)
    specs = [full(a) for a in pieces]
    for array, block, index, _, _ in terms:
        operands.append(array)
        specs.append(pl.BlockSpec(block, lambda i, index=index: index(i + first_tile)))
    if mask is not None:
        operands.append(mask)
        specs.append(full(mask))
    if add is not None:
        operands.append(add)
        specs.append(pl.BlockSpec((row_tile, n), lambda i: (i + first_tile, 0)))
    if separate:
        shape = (len(terms), rows, n)
        out_spec = pl.BlockSpec((len(terms), row_tile, n), lambda i: (0, i, 0))
    else:
        shape = (rows, n)
        out_spec = pl.BlockSpec((row_tile, n), lambda i: (i, 0))
    work = sum(rows * t[4] for t in terms)
    return pl.pallas_call(
        functools.partial(
            kernel_body, tuple((t[3], t[4]) for t in terms), mask is not None, add is not None, separate, leafwise
        ),
        out_shape=jax.ShapeDtypeStruct(shape, F32),
        grid_spec=pltpu.PrefetchScalarGridSpec(
            num_scalar_prefetch=0,
            grid=(steps,),
            in_specs=specs,
            out_specs=out_spec,
            scratch_shapes=[pltpu.VMEM((4 * PIECE, 2 * n), BF16)],
        ),
        compiler_params=pltpu.CompilerParams(vmem_limit_bytes=32 << 20),
        cost_estimate=pl.CostEstimate(flops=8 * work * n, bytes_accessed=4 * work, transcendentals=0),
    )(*operands)


def own_mask(pattern, rows, cols):
    r, c = lax.axis_index("rows"), lax.axis_index("cols")
    tr, tc = rows // TILE, cols // TILE
    part = lax.dynamic_slice(pattern, (0, r * tr, c * tc), (pattern.shape[0], tr, tc))
    return jnp.repeat(part.astype(F32), TILE, axis=2)


def grid_body(
    right_leaf,
    right_mid,
    right_root,
    inverse_leaf,
    inverse_mid,
    inverse_root,
    leaf_to_mid,
    leaf_to_root,
    mid_to_root,
    mask_leaf_mid,
    mask_leaf_root,
    mask_mid_root,
):
    k = place()[3]
    n = right_root.shape[-1]
    mask_lm = own_mask(mask_leaf_mid, *leaf_to_mid.shape[1:])
    mask_lr = own_mask(mask_leaf_root, *leaf_to_root.shape[1:])
    mask_mr = own_mask(mask_mid_root, *mid_to_root.shape[1:])
    pair = lambda a, tile, s: [
        (a, (1, tile, a.shape[2]), lambda i, l=l: (2 * s + l, i, 0), 2 * PIECE * l, a.shape[2]) for l in (0, 1)
    ]
    one = lambda a, tile, s: [(a, (1, tile, a.shape[2]), lambda i: (s, i, 0), 0, a.shape[2])]

    streams = (0, 1)
    first = [spread(lax.dynamic_index_in_dim(right_leaf, 2 * s + k, 0, False)) for s in streams]
    leaf_half, leaf_pieces = [], []
    for s in streams:
        part = apply(first[s], pair(inverse_leaf, 128, s), 256, 128, separate=True, leafwise=True)
        mine, other = halve(part)
        leaf_half.append(mine + other)
    leaf_pieces = [spread(h) for h in leaf_half]
    solved_leaf = [both_halves(h) for h in leaf_half]

    mid_half = []
    for s in streams:
        part = apply(
            leaf_pieces[s], pair(leaf_to_mid, 256, s), 512, 256, mask=mask_lm[2 * s : 2 * s + 2], leafwise=True
        )
        mine, other = halve(part.reshape(2, PIECE, n))
        right = lax.dynamic_index_in_dim(right_mid[s].reshape(2, PIECE, n), k, 0, False)
        mid_half.append(right - (mine + other))
    resid_pieces = [spread(h) for h in mid_half]

    root_part = None
    for s in streams:
        root_part = apply(
            leaf_pieces[s],
            pair(leaf_to_root, 256, s),
            1024,
            256,
            mask=mask_lr[2 * s : 2 * s + 2],
            add=root_part,
            leafwise=True,
        )

    solved_half = []
    for s in streams:
        part = apply(resid_pieces[s], one(inverse_mid, 256, s), 512, 256)
        mine, other = halve(part.reshape(2, PIECE, n))
        solved_half.append(mine + other)
    mid_pieces = [spread(h) for h in solved_half]
    solved_mid = [both_halves(h) for h in solved_half]

    root_part = apply(
        mid_pieces[0], one(mid_to_root, 256, 0), 1024, 256, mask=mask_mr[0:1], add=root_part
    )
    root_half = []
    for g in (0, 1):
        part = apply(
            mid_pieces[1],
            one(mid_to_root, 256, 1),
            512,
            256,
            first_tile=2 * g,
            mask=mask_mr[1:2, 4 * g : 4 * g + 4],
            add=root_part,
        )
        mine, other = halve(part.reshape(2, PIECE, n))
        right = lax.dynamic_index_in_dim(right_root.reshape(4, PIECE, n), 2 * g + k, 0, False)
        root_half.append(right - (mine + other))
    root_pieces = [spread(h) for h in root_half]

    columns = lambda g: [
        (inverse_root, (256, 512), lambda i, b=b: (i, 2 * b + g), 2 * PIECE * b, 2 * PIECE) for b in (0, 1)
    ]
    part = apply(root_pieces[0], columns(0), 1024, 256)
    solved_root = []
    for g in (0, 1):
        final = apply(root_pieces[1], columns(1), 512, 256, first_tile=2 * g, add=part)
        mine, other = halve(final.reshape(2, PIECE, n))
        solved_root.append(both_halves(mine + other))
    return (
        jnp.concatenate(solved_leaf, axis=0),
        jnp.stack([h.reshape(2 * PIECE, n) for h in solved_mid]),
        jnp.concatenate([h.reshape(2 * PIECE, n) for h in solved_root], axis=0),
    )


def body(*args):
    if lax.axis_size("rows") == 8 and lax.axis_size("cols") == 4 and args[0].shape == (4, PIECE, TILE):
        return grid_body(*args)
    return general_body(*args)


def solution(mesh):
    placed = (
        P(None, "rows", None),
        P(None, "rows", None),
        P("rows", None),
        P(None, "rows", "cols"),
        P(None, "rows", "cols"),
        P("rows", "cols"),
        P(None, "rows", "cols"),
        P(None, "rows", "cols"),
        P(None, "rows", "cols"),
        P(),
        P(),
        P(),
    )
    return jax.shard_map(
        body,
        mesh=mesh,
        in_specs=placed,
        out_specs=(P(None, "rows", None), P(None, "rows", None), P("rows", None)),
        check_vma=False,
    )
```

```python
import functools

import jax
import jax.numpy as jnp
from jax import lax
from jax.experimental import pallas as pl
from jax.experimental.pallas import tpu as pltpu
from jax.sharding import PartitionSpec as P

TILE = 128
AXES = ("rows", "cols")
BF16 = jnp.bfloat16
F32 = jnp.float32


def product(matrix, vector):
    return jnp.einsum(
        "src,sck->srk",
        matrix,
        vector,
        precision=lax.Precision.HIGHEST,
        preferred_element_type=jnp.float32,
    )


def masked(values, pattern):
    rows_dev = values.shape[1]
    cols_dev = values.shape[2]
    row_ids = lax.axis_index("rows") * rows_dev + lax.iota(jnp.int32, rows_dev)
    col_ids = lax.axis_index("cols") * cols_dev + lax.iota(jnp.int32, cols_dev)
    row_hot = (row_ids[:, None] // TILE == lax.iota(jnp.int32, pattern.shape[1])[None, :]).astype(F32)
    col_hot = (col_ids[:, None] // TILE == lax.iota(jnp.int32, pattern.shape[2])[None, :]).astype(F32)
    return values * jnp.einsum("ra,sab,cb->src", row_hot, pattern.astype(F32), col_hot)


def fetch_columns(block):
    gathered = lax.all_gather(block, "rows", axis=1, tiled=True)
    col_width = gathered.shape[1] // lax.axis_size("cols")
    return lax.dynamic_slice_in_dim(gathered, lax.axis_index("cols") * col_width, col_width, 1)


def general_body(
    right_leaf,
    right_mid,
    right_root,
    inverse_leaf,
    inverse_mid,
    inverse_root,
    leaf_to_mid,
    leaf_to_root,
    mid_to_root,
    mask_leaf_mid,
    mask_leaf_root,
    mask_mid_root,
):
    factor_lm = masked(leaf_to_mid, mask_leaf_mid)
    factor_lr = masked(leaf_to_root, mask_leaf_root)
    factor_mr = masked(mid_to_root, mask_mid_root)
    solved_leaf = lax.psum(product(inverse_leaf, fetch_columns(right_leaf)), "cols")
    leaf_columns = fetch_columns(solved_leaf)
    terms = product(factor_lm, leaf_columns)
    mid_part = terms.reshape(2, 2, terms.shape[1], terms.shape[2]).sum(axis=1)
    resid_mid = right_mid - lax.psum(mid_part, "cols")
    solved_mid = lax.psum(product(inverse_mid, fetch_columns(resid_mid)), "cols")
    mid_columns = fetch_columns(solved_mid)
    root_part = product(factor_lr, leaf_columns).sum(axis=0) + product(factor_mr, mid_columns).sum(axis=0)
    resid_root = right_root - lax.psum(root_part, "cols")
    solved_root = lax.psum(product(inverse_root[None], fetch_columns(resid_root[None])), "cols")
    return (solved_leaf, solved_mid, solved_root[0])


PIECE = 256


def flat(x, y, z, k):
    return (2 * z + y) * 4 + 2 * x + k


PLACES = [(x, y, z, k) for x in (0, 1) for y in (0, 1) for z in range(4) for k in (0, 1)]
TO_CORE = [(flat(x, y, z, k), flat(x, y, z, 1 - k)) for x, y, z, k in PLACES]
TO_X = [(flat(x, y, z, k), flat(1 - x, y, z, k)) for x, y, z, k in PLACES]
TO_Y = [(flat(x, y, z, k), flat(x, 1 - y, z, k)) for x, y, z, k in PLACES]
TO_Z = [(flat(x, y, z, k), flat(x, y, z ^ 1, k)) for x, y, z, k in PLACES]
TO_YZ = [(flat(x, y, z, k), flat(x, 1 - y, z ^ 1, k)) for x, y, z, k in PLACES]
TO_FAR = [(flat(x, y, z, k), flat(x, y, z ^ 2, k)) for x, y, z, k in PLACES if z // 2 == x]


def send(value, pairs):
    return lax.ppermute(value, AXES, pairs)


def place():
    r, c = lax.axis_index("rows"), lax.axis_index("cols")
    return c // 2, r % 2, r // 2, c % 2


def halve(part):
    k = place()[3]
    other = send(part, TO_CORE)
    mine = lax.dynamic_index_in_dim(part, k, 0, False) + lax.dynamic_index_in_dim(other, k, 0, False)
    return mine, send(mine, TO_X)


def both_halves(mine):
    k = place()[3]
    other = send(mine, TO_CORE)
    first = k == 0
    return jnp.stack([jnp.where(first, mine, other), jnp.where(first, other, mine)])


def spread(mine):
    x, y, z, k = place()
    far = send(mine, TO_FAR)
    own = jnp.where(z // 2 == x, mine, far)
    beside, above = send(own, TO_Y), send(own, TO_Z)
    across = send(above, TO_Y)
    same = (z % 2) == k
    swapped = send(jnp.stack([jnp.where(same, above, own), jnp.where(same, across, beside)]), TO_CORE)
    return own, beside, above, across, swapped


def split(value):
    high = value.astype(BF16)
    return high, (value - high.astype(F32)).astype(BF16)


def kernel_body(spans, has_mask, has_add, separate, leafwise, *refs):
    own, beside, above, across, swapped = refs[:5]
    refs = refs[5:]
    count = len(spans)
    mats, refs = refs[:count], refs[count:]
    if has_mask:
        mask, refs = refs[0], refs[1:]
    if has_add:
        add, refs = refs[0], refs[1:]
    out, held = refs
    step = pl.program_id(0)
    n = out.shape[-1]

    @pl.when(step == 0)
    def _():
        r, c = lax.axis_index("rows"), lax.axis_index("cols")
        y, k = lax.rem(r, 2), lax.rem(c, 2)
        same = lax.rem(r // 2, 2) == k

        def put(value, y_of, half):
            row = half * (2 * PIECE) + y_of * PIECE if leafwise else y_of * (2 * PIECE) + half * PIECE
            row = pl.multiple_of(row, PIECE)
            high, low = split(value)
            held[pl.ds(row, PIECE), :n] = high
            held[pl.ds(row, PIECE), n:] = low

        @pl.when(same)
        def _():
            put(own[...], y, k)
            put(beside[...], 1 - y, k)

        @pl.when(jnp.logical_not(same))
        def _():
            put(above[...], y, k)
            put(across[...], 1 - y, k)

        put(swapped[0], y, 1 - k)
        put(swapped[1], 1 - y, 1 - k)

    total = None
    for t, (start, width) in enumerate(spans):
        leaf = t if len(mats) == 1 or mats[t].ndim == 3 else 0
        a = mats[t][0] if mats[t].ndim == 3 else mats[t][...]
        if has_mask:
            rows = a.shape[0] // TILE
            a = jnp.concatenate(
                [a[q * TILE : (q + 1) * TILE] * mask[t, pl.ds(step * rows + q, 1), :] for q in range(rows)], axis=0
            )
        high, low = split(a)
        x = held[start : start + width, :]
        wide = jnp.dot(high, x, preferred_element_type=F32)
        value = jnp.dot(low, x[:, :n], preferred_element_type=F32) + wide[:, n:] + wide[:, :n]
        if separate:
            out[t] = value
        else:
            total = value if total is None else total + value
    if not separate:
        if has_add:
            total = total + add[...]
        out[...] = total


def apply(pieces, terms, rows, row_tile, first_tile=0, mask=None, add=None, separate=False, leafwise=False):
    n = pieces[0].shape[-1]
    steps = rows // row_tile
    full = lambda a: pl.BlockSpec(a.shape, lambda i, d=a.ndim: (0,) * d)
    operands = list(pieces)
    specs = [full(a) for a in pieces]
    for array, block, index, _, _ in terms:
        operands.append(array)
        specs.append(pl.BlockSpec(block, lambda i, index=index: index(i + first_tile)))
    if mask is not None:
        operands.append(mask)
        specs.append(full(mask))
    if add is not None:
        operands.append(add)
        specs.append(pl.BlockSpec((row_tile, n), lambda i: (i + first_tile, 0)))
    if separate:
        shape = (len(terms), rows, n)
        out_spec = pl.BlockSpec((len(terms), row_tile, n), lambda i: (0, i, 0))
    else:
        shape = (rows, n)
        out_spec = pl.BlockSpec((row_tile, n), lambda i: (i, 0))
    work = sum(rows * t[4] for t in terms)
    return pl.pallas_call(
        functools.partial(
            kernel_body, tuple((t[3], t[4]) for t in terms), mask is not None, add is not None, separate, leafwise
        ),
        out_shape=jax.ShapeDtypeStruct(shape, F32),
        grid_spec=pltpu.PrefetchScalarGridSpec(
            num_scalar_prefetch=0,
            grid=(steps,),
            in_specs=specs,
            out_specs=out_spec,
            scratch_shapes=[pltpu.VMEM((4 * PIECE, 2 * n), BF16)],
        ),
        compiler_params=pltpu.CompilerParams(vmem_limit_bytes=32 << 20),
        cost_estimate=pl.CostEstimate(flops=8 * work * n, bytes_accessed=4 * work, transcendentals=0),
    )(*operands)


def own_mask(pattern, rows, cols):
    r, c = lax.axis_index("rows"), lax.axis_index("cols")
    tr, tc = rows // TILE, cols // TILE
    part = lax.dynamic_slice(pattern, (0, r * tr, c * tc), (pattern.shape[0], tr, tc))
    return jnp.repeat(part.astype(F32), TILE, axis=2)


def grid_body(
    right_leaf,
    right_mid,
    right_root,
    inverse_leaf,
    inverse_mid,
    inverse_root,
    leaf_to_mid,
    leaf_to_root,
    mid_to_root,
    mask_leaf_mid,
    mask_leaf_root,
    mask_mid_root,
):
    k = place()[3]
    n = right_root.shape[-1]
    mask_lm = own_mask(mask_leaf_mid, *leaf_to_mid.shape[1:])
    mask_lr = own_mask(mask_leaf_root, *leaf_to_root.shape[1:])
    mask_mr = own_mask(mask_mid_root, *mid_to_root.shape[1:])
    pair = lambda a, tile, s: [
        (a, (1, tile, a.shape[2]), lambda i, l=l: (2 * s + l, i, 0), 2 * PIECE * l, a.shape[2]) for l in (0, 1)
    ]
    one = lambda a, tile, s: [(a, (1, tile, a.shape[2]), lambda i: (s, i, 0), 0, a.shape[2])]

    streams = (0, 1)
    first = [spread(lax.dynamic_index_in_dim(right_leaf, 2 * s + k, 0, False)) for s in streams]
    leaf_half, leaf_pieces = [], []
    for s in streams:
        part = apply(first[s], pair(inverse_leaf, 128, s), 256, 128, separate=True, leafwise=True)
        mine, other = halve(part)
        leaf_half.append(mine + other)
    leaf_pieces = [spread(h) for h in leaf_half]
    solved_leaf = [both_halves(h) for h in leaf_half]

    mid_half = []
    for s in streams:
        part = apply(
            leaf_pieces[s], pair(leaf_to_mid, 256, s), 512, 256, mask=mask_lm[2 * s : 2 * s + 2], leafwise=True
        )
        mine, other = halve(part.reshape(2, PIECE, n))
        right = lax.dynamic_index_in_dim(right_mid[s].reshape(2, PIECE, n), k, 0, False)
        mid_half.append(right - (mine + other))
    resid_pieces = [spread(h) for h in mid_half]

    root_part = None
    for s in streams:
        root_part = apply(
            leaf_pieces[s],
            pair(leaf_to_root, 256, s),
            1024,
            256,
            mask=mask_lr[2 * s : 2 * s + 2],
            add=root_part,
            leafwise=True,
        )

    solved_half = []
    for s in streams:
        part = apply(resid_pieces[s], one(inverse_mid, 256, s), 512, 256)
        mine, other = halve(part.reshape(2, PIECE, n))
        solved_half.append(mine + other)
    mid_pieces = [spread(h) for h in solved_half]
    solved_mid = [both_halves(h) for h in solved_half]

    root_part = apply(
        mid_pieces[0], one(mid_to_root, 256, 0), 1024, 256, mask=mask_mr[0:1], add=root_part
    )
    root_half = []
    for g in (0, 1):
        part = apply(
            mid_pieces[1],
            one(mid_to_root, 256, 1),
            512,
            256,
            first_tile=2 * g,
            mask=mask_mr[1:2, 4 * g : 4 * g + 4],
            add=root_part,
        )
        mine, other = halve(part.reshape(2, PIECE, n))
        right = lax.dynamic_index_in_dim(right_root.reshape(4, PIECE, n), 2 * g + k, 0, False)
        root_half.append(right - (mine + other))
    root_pieces = [spread(h) for h in root_half]

    columns = lambda g: [
        (inverse_root, (256, 512), lambda i, b=b: (i, 2 * b + g), 2 * PIECE * b, 2 * PIECE) for b in (0, 1)
    ]
    part = apply(root_pieces[0], columns(0), 1024, 256)
    mine, theirs = [], []
    for g in (0, 1):
        final = apply(root_pieces[1], columns(1), 512, 256, first_tile=2 * g, add=part)
        one_half, other = halve(final.reshape(2, PIECE, n))
        mine.append(one_half + other)
        theirs.append(send(mine[g], TO_CORE))
    first_group = lax.broadcasted_iota(jnp.int32, (2, 2, 1, 1), 0) == 0
    here = lax.broadcasted_iota(jnp.int32, (2, 2, 1, 1), 1) == k
    solved_root = jnp.where(
        here, jnp.where(first_group, mine[0], mine[1]), jnp.where(first_group, theirs[0], theirs[1])
    ).reshape(4 * PIECE, n)
    return (
        jnp.concatenate(solved_leaf, axis=0),
        jnp.stack([h.reshape(2 * PIECE, n) for h in solved_mid]),
        solved_root,
    )


def body(*args):
    if lax.axis_size("rows") == 8 and lax.axis_size("cols") == 4 and args[0].shape == (4, PIECE, TILE):
        return grid_body(*args)
    return general_body(*args)


def solution(mesh):
    placed = (
        P(None, "rows", None),
        P(None, "rows", None),
        P("rows", None),
        P(None, "rows", "cols"),
        P(None, "rows", "cols"),
        P("rows", "cols"),
        P(None, "rows", "cols"),
        P(None, "rows", "cols"),
        P(None, "rows", "cols"),
        P(),
        P(),
        P(),
    )
    return jax.shard_map(
        body,
        mesh=mesh,
        in_specs=placed,
        out_specs=(P(None, "rows", None), P(None, "rows", None), P("rows", None)),
        check_vma=False,
    )
```

```python
import functools

import jax
import jax.numpy as jnp
from jax import lax
from jax.experimental import pallas as pl
from jax.experimental.pallas import tpu as pltpu
from jax.sharding import PartitionSpec as P

TILE = 128
AXES = ("rows", "cols")
BF16 = jnp.bfloat16
F32 = jnp.float32


def product(matrix, vector):
    return jnp.einsum(
        "src,sck->srk",
        matrix,
        vector,
        precision=lax.Precision.HIGHEST,
        preferred_element_type=jnp.float32,
    )


def masked(values, pattern):
    rows_dev = values.shape[1]
    cols_dev = values.shape[2]
    row_ids = lax.axis_index("rows") * rows_dev + lax.iota(jnp.int32, rows_dev)
    col_ids = lax.axis_index("cols") * cols_dev + lax.iota(jnp.int32, cols_dev)
    row_hot = (row_ids[:, None] // TILE == lax.iota(jnp.int32, pattern.shape[1])[None, :]).astype(F32)
    col_hot = (col_ids[:, None] // TILE == lax.iota(jnp.int32, pattern.shape[2])[None, :]).astype(F32)
    return values * jnp.einsum("ra,sab,cb->src", row_hot, pattern.astype(F32), col_hot)


def fetch_columns(block):
    gathered = lax.all_gather(block, "rows", axis=1, tiled=True)
    col_width = gathered.shape[1] // lax.axis_size("cols")
    return lax.dynamic_slice_in_dim(gathered, lax.axis_index("cols") * col_width, col_width, 1)


def general_body(
    right_leaf,
    right_mid,
    right_root,
    inverse_leaf,
    inverse_mid,
    inverse_root,
    leaf_to_mid,
    leaf_to_root,
    mid_to_root,
    mask_leaf_mid,
    mask_leaf_root,
    mask_mid_root,
):
    factor_lm = masked(leaf_to_mid, mask_leaf_mid)
    factor_lr = masked(leaf_to_root, mask_leaf_root)
    factor_mr = masked(mid_to_root, mask_mid_root)
    solved_leaf = lax.psum(product(inverse_leaf, fetch_columns(right_leaf)), "cols")
    leaf_columns = fetch_columns(solved_leaf)
    terms = product(factor_lm, leaf_columns)
    mid_part = terms.reshape(2, 2, terms.shape[1], terms.shape[2]).sum(axis=1)
    resid_mid = right_mid - lax.psum(mid_part, "cols")
    solved_mid = lax.psum(product(inverse_mid, fetch_columns(resid_mid)), "cols")
    mid_columns = fetch_columns(solved_mid)
    root_part = product(factor_lr, leaf_columns).sum(axis=0) + product(factor_mr, mid_columns).sum(axis=0)
    resid_root = right_root - lax.psum(root_part, "cols")
    solved_root = lax.psum(product(inverse_root[None], fetch_columns(resid_root[None])), "cols")
    return (solved_leaf, solved_mid, solved_root[0])


PIECE = 256


def flat(x, y, z, k):
    return (2 * z + y) * 4 + 2 * x + k


PLACES = [(x, y, z, k) for x in (0, 1) for y in (0, 1) for z in range(4) for k in (0, 1)]
TO_CORE = [(flat(x, y, z, k), flat(x, y, z, 1 - k)) for x, y, z, k in PLACES]
TO_X = [(flat(x, y, z, k), flat(1 - x, y, z, k)) for x, y, z, k in PLACES]
TO_Y = [(flat(x, y, z, k), flat(x, 1 - y, z, k)) for x, y, z, k in PLACES]
TO_Z = [(flat(x, y, z, k), flat(x, y, z ^ 1, k)) for x, y, z, k in PLACES]
TO_YZ = [(flat(x, y, z, k), flat(x, 1 - y, z ^ 1, k)) for x, y, z, k in PLACES]
TO_FAR = [(flat(x, y, z, k), flat(x, y, 3 - z, k)) for x, y, z, k in PLACES if z // 2 == x]


def send(value, pairs):
    return lax.ppermute(value, AXES, pairs)


def place():
    r, c = lax.axis_index("rows"), lax.axis_index("cols")
    return c // 2, r % 2, r // 2, c % 2


def halve(part):
    k = place()[3]
    other = send(part, TO_CORE)
    mine = lax.dynamic_index_in_dim(part, k, 0, False) + lax.dynamic_index_in_dim(other, k, 0, False)
    return mine, send(mine, TO_X)


def both_halves(mine):
    k = place()[3]
    other = send(mine, TO_CORE)
    first = k == 0
    return jnp.stack([jnp.where(first, mine, other), jnp.where(first, other, mine)])


def gate(value, after):
    return lax.optimization_barrier((value, after))[0]


def spread(mine, make=None):
    x, y, z, k = place()
    far = send(mine, TO_FAR)
    own = jnp.where(z // 2 == x, mine, far)
    made = None
    if make is not None:
        made = make(mine)
        own = gate(own, made)
    beside, above = send(own, TO_Y), send(own, TO_Z)
    across = send(above, TO_Y)
    same = jnp.where(z // 2 == x, z % 2, 1 - z % 2) == k
    swapped = send(jnp.stack([jnp.where(same, above, own), jnp.where(same, across, beside)]), TO_CORE)
    pieces = (own, beside, above, across, swapped)
    return pieces if make is None else (pieces, made)


def split(value):
    high = value.astype(BF16)
    return high, (value - high.astype(F32)).astype(BF16)


def kernel_body(spans, has_mask, has_add, separate, leafwise, *refs):
    own, beside, above, across, swapped = refs[:5]
    refs = refs[5:]
    count = len(spans)
    mats, refs = refs[:count], refs[count:]
    if has_mask:
        mask, refs = refs[0], refs[1:]
    if has_add:
        add, refs = refs[0], refs[1:]
    out, held = refs
    step = pl.program_id(0)
    n = out.shape[-1]

    @pl.when(step == 0)
    def _():
        r, c = lax.axis_index("rows"), lax.axis_index("cols")
        y, k = lax.rem(r, 2), lax.rem(c, 2)
        z = r // 2
        same = jnp.where(z // 2 == c // 2, lax.rem(z, 2), 1 - lax.rem(z, 2)) == k

        def put(value, y_of, half):
            row = half * (2 * PIECE) + y_of * PIECE if leafwise else y_of * (2 * PIECE) + half * PIECE
            row = pl.multiple_of(row, PIECE)
            high, low = split(value)
            held[pl.ds(row, PIECE), :n] = high
            held[pl.ds(row, PIECE), n:] = low

        @pl.when(same)
        def _():
            put(own[...], y, k)
            put(beside[...], 1 - y, k)

        @pl.when(jnp.logical_not(same))
        def _():
            put(above[...], y, k)
            put(across[...], 1 - y, k)

        put(swapped[0], y, 1 - k)
        put(swapped[1], 1 - y, 1 - k)

    total = None
    for t, (start, width) in enumerate(spans):
        leaf = t if len(mats) == 1 or mats[t].ndim == 3 else 0
        a = mats[t][0] if mats[t].ndim == 3 else mats[t][...]
        if has_mask:
            rows = a.shape[0] // TILE
            a = jnp.concatenate(
                [a[q * TILE : (q + 1) * TILE] * mask[t, pl.ds(step * rows + q, 1), :] for q in range(rows)], axis=0
            )
        high, low = split(a)
        x = held[start : start + width, :]
        wide = jnp.dot(high, x, preferred_element_type=F32)
        value = jnp.dot(low, x[:, :n], preferred_element_type=F32) + wide[:, n:] + wide[:, :n]
        if separate:
            out[t] = value
        else:
            total = value if total is None else total + value
    if not separate:
        if has_add:
            total = total + add[...]
        out[...] = total


def apply(pieces, terms, rows, row_tile, first_tile=0, mask=None, add=None, separate=False, leafwise=False):
    n = pieces[0].shape[-1]
    steps = rows // row_tile
    full = lambda a: pl.BlockSpec(a.shape, lambda i, d=a.ndim: (0,) * d)
    operands = list(pieces)
    specs = [full(a) for a in pieces]
    for array, block, index, _, _ in terms:
        operands.append(array)
        specs.append(pl.BlockSpec(block, lambda i, index=index: index(i + first_tile)))
    if mask is not None:
        operands.append(mask)
        specs.append(full(mask))
    if add is not None:
        operands.append(add)
        specs.append(pl.BlockSpec((row_tile, n), lambda i: (i + first_tile, 0)))
    if separate:
        shape = (len(terms), rows, n)
        out_spec = pl.BlockSpec((len(terms), row_tile, n), lambda i: (0, i, 0))
    else:
        shape = (rows, n)
        out_spec = pl.BlockSpec((row_tile, n), lambda i: (i, 0))
    work = sum(rows * t[4] for t in terms)
    return pl.pallas_call(
        functools.partial(
            kernel_body, tuple((t[3], t[4]) for t in terms), mask is not None, add is not None, separate, leafwise
        ),
        out_shape=jax.ShapeDtypeStruct(shape, F32),
        grid_spec=pltpu.PrefetchScalarGridSpec(
            num_scalar_prefetch=0,
            grid=(steps,),
            in_specs=specs,
            out_specs=out_spec,
            scratch_shapes=[pltpu.VMEM((4 * PIECE, 2 * n), BF16)],
        ),
        compiler_params=pltpu.CompilerParams(vmem_limit_bytes=32 << 20),
        cost_estimate=pl.CostEstimate(flops=8 * work * n, bytes_accessed=4 * work, transcendentals=0),
    )(*operands)


def own_mask(pattern, rows, cols):
    r, c = lax.axis_index("rows"), lax.axis_index("cols")
    tr, tc = rows // TILE, cols // TILE
    part = lax.dynamic_slice(pattern, (0, r * tr, c * tc), (pattern.shape[0], tr, tc))
    return jnp.repeat(part.astype(F32), TILE, axis=2)


def grid_body(
    right_leaf,
    right_mid,
    right_root,
    inverse_leaf,
    inverse_mid,
    inverse_root,
    leaf_to_mid,
    leaf_to_root,
    mid_to_root,
    mask_leaf_mid,
    mask_leaf_root,
    mask_mid_root,
):
    k = place()[3]
    n = right_root.shape[-1]
    mask_lm = own_mask(mask_leaf_mid, *leaf_to_mid.shape[1:])
    mask_lr = own_mask(mask_leaf_root, *leaf_to_root.shape[1:])
    mask_mr = own_mask(mask_mid_root, *mid_to_root.shape[1:])
    pair = lambda a, tile, s: [
        (a, (1, tile, a.shape[2]), lambda i, l=l: (2 * s + l, i, 0), 2 * PIECE * l, a.shape[2]) for l in (0, 1)
    ]
    one = lambda a, tile, s: [(a, (1, tile, a.shape[2]), lambda i: (s, i, 0), 0, a.shape[2])]

    streams = (0, 1)
    first = [spread(lax.dynamic_index_in_dim(right_leaf, 2 * s + k, 0, False)) for s in streams]
    leaf_half, leaf_pieces = [], []
    for s in streams:
        part = apply(first[s], pair(inverse_leaf, 128, s), 256, 128, separate=True, leafwise=True)
        mine, other = halve(part)
        leaf_half.append(mine + other)
    leaf_pieces = [spread(h) for h in leaf_half]
    solved_leaf = [both_halves(h) for h in leaf_half]

    mid_half = []
    for s in streams:
        part = apply(
            leaf_pieces[s], pair(leaf_to_mid, 256, s), 512, 256, mask=mask_lm[2 * s : 2 * s + 2], leafwise=True
        )
        mine, other = halve(part.reshape(2, PIECE, n))
        right = lax.dynamic_index_in_dim(right_mid[s].reshape(2, PIECE, n), k, 0, False)
        mid_half.append(right - (mine + other))
    root_part, resid_pieces = None, []
    for s in streams:

        def make(mine, s=s, before=root_part):
            p = leaf_pieces[s]
            return apply(
                (gate(p[0], mine),) + p[1:],
                [(pltpu.with_memory_space_constraint(t[0], pltpu.MemorySpace.HBM),) + t[1:] for t in pair(leaf_to_root, 256, s)],
                1024,
                256,
                mask=mask_lr[2 * s : 2 * s + 2],
                add=before,
                leafwise=True,
            )

        pieces, root_part = spread(mid_half[s], make)
        resid_pieces.append(pieces)

    solved_half = []
    for s in streams:
        part = apply(resid_pieces[s], one(inverse_mid, 256, s), 512, 256)
        mine, other = halve(part.reshape(2, PIECE, n))
        solved_half.append(mine + other)
    mid_pieces = [spread(h) for h in solved_half]
    solved_mid = [both_halves(h) for h in solved_half]

    root_part = apply(
        mid_pieces[0], one(mid_to_root[0:1], 256, 0), 1024, 256, mask=mask_mr[0:1], add=root_part
    )
    root_half = []
    for g in (0, 1):
        part = apply(
            mid_pieces[1],
            one(mid_to_root[1:2], 256, 0),
            512,
            256,
            first_tile=2 * g,
            mask=mask_mr[1:2, 4 * g : 4 * g + 4],
            add=root_part,
        )
        mine, other = halve(part.reshape(2, PIECE, n))
        right = lax.dynamic_index_in_dim(right_root.reshape(4, PIECE, n), 2 * g + k, 0, False)
        root_half.append(right - (mine + other))
    root_pieces = [spread(h) for h in root_half]

    columns = lambda g: [
        (inverse_root, (256, 512), lambda i, b=b: (i, 2 * b + g), 2 * PIECE * b, 2 * PIECE) for b in (0, 1)
    ]
    part = apply(root_pieces[0], columns(0), 1024, 256)
    mine, theirs = [], []
    for g in (0, 1):
        final = apply(root_pieces[1], columns(1), 512, 256, first_tile=2 * g, add=part)
        one_half, other = halve(final.reshape(2, PIECE, n))
        mine.append(one_half + other)
        theirs.append(send(mine[g], TO_CORE))
    first_group = lax.broadcasted_iota(jnp.int32, (2, 2, 1, 1), 0) == 0
    here = lax.broadcasted_iota(jnp.int32, (2, 2, 1, 1), 1) == k
    solved_root = jnp.where(
        here, jnp.where(first_group, mine[0], mine[1]), jnp.where(first_group, theirs[0], theirs[1])
    ).reshape(4 * PIECE, n)
    return (
        jnp.concatenate(solved_leaf, axis=0),
        jnp.stack([h.reshape(2 * PIECE, n) for h in solved_mid]),
        solved_root,
    )


def body(*args):
    if lax.axis_size("rows") == 8 and lax.axis_size("cols") == 4 and args[0].shape == (4, PIECE, TILE):
        return grid_body(*args)
    return general_body(*args)


def solution(mesh):
    placed = (
        P(None, "rows", None),
        P(None, "rows", None),
        P("rows", None),
        P(None, "rows", "cols"),
        P(None, "rows", "cols"),
        P("rows", "cols"),
        P(None, "rows", "cols"),
        P(None, "rows", "cols"),
        P(None, "rows", "cols"),
        P(),
        P(),
        P(),
    )
    return jax.shard_map(
        body,
        mesh=mesh,
        in_specs=placed,
        out_specs=(P(None, "rows", None), P(None, "rows", None), P("rows", None)),
        check_vma=False,
    )
```

```python
import functools

import jax
import jax.numpy as jnp
from jax import lax
from jax.experimental import pallas as pl
from jax.experimental.pallas import tpu as pltpu
from jax.sharding import PartitionSpec as P

TILE = 128
AXES = ("rows", "cols")
BF16 = jnp.bfloat16
F32 = jnp.float32


def product(matrix, vector):
    return jnp.einsum(
        "src,sck->srk",
        matrix,
        vector,
        precision=lax.Precision.HIGHEST,
        preferred_element_type=jnp.float32,
    )


def masked(values, pattern):
    rows_dev = values.shape[1]
    cols_dev = values.shape[2]
    row_ids = lax.axis_index("rows") * rows_dev + lax.iota(jnp.int32, rows_dev)
    col_ids = lax.axis_index("cols") * cols_dev + lax.iota(jnp.int32, cols_dev)
    row_hot = (row_ids[:, None] // TILE == lax.iota(jnp.int32, pattern.shape[1])[None, :]).astype(F32)
    col_hot = (col_ids[:, None] // TILE == lax.iota(jnp.int32, pattern.shape[2])[None, :]).astype(F32)
    return values * jnp.einsum("ra,sab,cb->src", row_hot, pattern.astype(F32), col_hot)


def fetch_columns(block):
    gathered = lax.all_gather(block, "rows", axis=1, tiled=True)
    col_width = gathered.shape[1] // lax.axis_size("cols")
    return lax.dynamic_slice_in_dim(gathered, lax.axis_index("cols") * col_width, col_width, 1)


def general_body(
    right_leaf,
    right_mid,
    right_root,
    inverse_leaf,
    inverse_mid,
    inverse_root,
    leaf_to_mid,
    leaf_to_root,
    mid_to_root,
    mask_leaf_mid,
    mask_leaf_root,
    mask_mid_root,
):
    factor_lm = masked(leaf_to_mid, mask_leaf_mid)
    factor_lr = masked(leaf_to_root, mask_leaf_root)
    factor_mr = masked(mid_to_root, mask_mid_root)
    solved_leaf = lax.psum(product(inverse_leaf, fetch_columns(right_leaf)), "cols")
    leaf_columns = fetch_columns(solved_leaf)
    terms = product(factor_lm, leaf_columns)
    mid_part = terms.reshape(2, 2, terms.shape[1], terms.shape[2]).sum(axis=1)
    resid_mid = right_mid - lax.psum(mid_part, "cols")
    solved_mid = lax.psum(product(inverse_mid, fetch_columns(resid_mid)), "cols")
    mid_columns = fetch_columns(solved_mid)
    root_part = product(factor_lr, leaf_columns).sum(axis=0) + product(factor_mr, mid_columns).sum(axis=0)
    resid_root = right_root - lax.psum(root_part, "cols")
    solved_root = lax.psum(product(inverse_root[None], fetch_columns(resid_root[None])), "cols")
    return (solved_leaf, solved_mid, solved_root[0])


PIECE = 256


def flat(x, y, z, k):
    return (2 * z + y) * 4 + 2 * x + k


PLACES = [(x, y, z, k) for x in (0, 1) for y in (0, 1) for z in range(4) for k in (0, 1)]
TO_CORE = [(flat(x, y, z, k), flat(x, y, z, 1 - k)) for x, y, z, k in PLACES]
TO_X = [(flat(x, y, z, k), flat(1 - x, y, z, k)) for x, y, z, k in PLACES]
TO_Y = [(flat(x, y, z, k), flat(x, 1 - y, z, k)) for x, y, z, k in PLACES]
TO_Z = [(flat(x, y, z, k), flat(x, y, z ^ 1, k)) for x, y, z, k in PLACES]
TO_YZ = [(flat(x, y, z, k), flat(x, 1 - y, z ^ 1, k)) for x, y, z, k in PLACES]
TO_FAR = [(flat(x, y, z, k), flat(x, y, 3 - z, k)) for x, y, z, k in PLACES if z // 2 == x]


def send(value, pairs):
    return lax.ppermute(value, AXES, pairs)


def place():
    r, c = lax.axis_index("rows"), lax.axis_index("cols")
    return c // 2, r % 2, r // 2, c % 2


def halve(part):
    k = place()[3]
    other = send(part, TO_CORE)
    mine = lax.dynamic_index_in_dim(part, k, 0, False) + lax.dynamic_index_in_dim(other, k, 0, False)
    return mine, send(mine, TO_X)


def both_halves(mine):
    k = place()[3]
    other = send(mine, TO_CORE)
    first = k == 0
    return jnp.stack([jnp.where(first, mine, other), jnp.where(first, other, mine)])


def gate(value, after):
    return lax.optimization_barrier((value, after))[0]


def spread(mine, make=None):
    x, y, z, k = place()
    far = send(mine, TO_FAR)
    own = jnp.where(z // 2 == x, mine, far)
    made = None
    if make is not None:
        made = make(mine)
        own = gate(own, made)
    beside, above, across = send(own, TO_Y), send(own, TO_Z), send(own, TO_YZ)
    same = jnp.where(z // 2 == x, z % 2, 1 - z % 2) == k
    swapped = send(jnp.stack([jnp.where(same, above, own), jnp.where(same, across, beside)]), TO_CORE)
    pieces = (own, beside, above, across, swapped)
    return pieces if make is None else (pieces, made)


def split(value):
    high = value.astype(BF16)
    return high, (value - high.astype(F32)).astype(BF16)


def kernel_body(spans, has_mask, has_add, separate, leafwise, *refs):
    own, beside, above, across, swapped = refs[:5]
    refs = refs[5:]
    count = len(spans)
    mats, refs = refs[:count], refs[count:]
    if has_mask:
        mask, refs = refs[0], refs[1:]
    if has_add:
        add, refs = refs[0], refs[1:]
    out, held = refs
    step = pl.program_id(0)
    n = out.shape[-1]

    @pl.when(step == 0)
    def _():
        r, c = lax.axis_index("rows"), lax.axis_index("cols")
        y, k = lax.rem(r, 2), lax.rem(c, 2)
        z = r // 2
        same = jnp.where(z // 2 == c // 2, lax.rem(z, 2), 1 - lax.rem(z, 2)) == k

        def put(value, y_of, half):
            row = half * (2 * PIECE) + y_of * PIECE if leafwise else y_of * (2 * PIECE) + half * PIECE
            row = pl.multiple_of(row, PIECE)
            high, low = split(value)
            held[pl.ds(row, PIECE), :n] = high
            held[pl.ds(row, PIECE), n:] = low

        @pl.when(same)
        def _():
            put(own[...], y, k)
            put(beside[...], 1 - y, k)

        @pl.when(jnp.logical_not(same))
        def _():
            put(above[...], y, k)
            put(across[...], 1 - y, k)

        put(swapped[0], y, 1 - k)
        put(swapped[1], 1 - y, 1 - k)

    total = None
    for t, (start, width) in enumerate(spans):
        leaf = t if len(mats) == 1 or mats[t].ndim == 3 else 0
        a = mats[t][0] if mats[t].ndim == 3 else mats[t][...]
        if has_mask:
            rows = a.shape[0] // TILE
            a = jnp.concatenate(
                [a[q * TILE : (q + 1) * TILE] * mask[t, pl.ds(step * rows + q, 1), :] for q in range(rows)], axis=0
            )
        high, low = split(a)
        x = held[start : start + width, :]
        wide = jnp.dot(high, x, preferred_element_type=F32)
        value = jnp.dot(low, x[:, :n], preferred_element_type=F32) + wide[:, n:] + wide[:, :n]
        if separate:
            out[t] = value
        else:
            total = value if total is None else total + value
    if not separate:
        if has_add:
            total = total + add[...]
        out[...] = total


def apply(pieces, terms, rows, row_tile, first_tile=0, mask=None, add=None, separate=False, leafwise=False):
    n = pieces[0].shape[-1]
    steps = rows // row_tile
    full = lambda a: pl.BlockSpec(a.shape, lambda i, d=a.ndim: (0,) * d)
    operands = list(pieces)
    specs = [full(a) for a in pieces]
    for array, block, index, _, _ in terms:
        operands.append(array)
        specs.append(pl.BlockSpec(block, lambda i, index=index: index(i + first_tile)))
    if mask is not None:
        operands.append(mask)
        specs.append(full(mask))
    if add is not None:
        operands.append(add)
        specs.append(pl.BlockSpec((row_tile, n), lambda i: (i + first_tile, 0)))
    if separate:
        shape = (len(terms), rows, n)
        out_spec = pl.BlockSpec((len(terms), row_tile, n), lambda i: (0, i, 0))
    else:
        shape = (rows, n)
        out_spec = pl.BlockSpec((row_tile, n), lambda i: (i, 0))
    work = sum(rows * t[4] for t in terms)
    return pl.pallas_call(
        functools.partial(
            kernel_body, tuple((t[3], t[4]) for t in terms), mask is not None, add is not None, separate, leafwise
        ),
        out_shape=jax.ShapeDtypeStruct(shape, F32),
        grid_spec=pltpu.PrefetchScalarGridSpec(
            num_scalar_prefetch=0,
            grid=(steps,),
            in_specs=specs,
            out_specs=out_spec,
            scratch_shapes=[pltpu.VMEM((4 * PIECE, 2 * n), BF16)],
        ),
        compiler_params=pltpu.CompilerParams(vmem_limit_bytes=32 << 20),
        cost_estimate=pl.CostEstimate(flops=8 * work * n, bytes_accessed=4 * work, transcendentals=0),
    )(*operands)


def own_mask(pattern, rows, cols):
    r, c = lax.axis_index("rows"), lax.axis_index("cols")
    tr, tc = rows // TILE, cols // TILE
    part = lax.dynamic_slice(pattern, (0, r * tr, c * tc), (pattern.shape[0], tr, tc))
    return jnp.repeat(part.astype(F32), TILE, axis=2)


def grid_body(
    right_leaf,
    right_mid,
    right_root,
    inverse_leaf,
    inverse_mid,
    inverse_root,
    leaf_to_mid,
    leaf_to_root,
    mid_to_root,
    mask_leaf_mid,
    mask_leaf_root,
    mask_mid_root,
):
    k = place()[3]
    n = right_root.shape[-1]
    mask_lm = own_mask(mask_leaf_mid, *leaf_to_mid.shape[1:])
    mask_lr = own_mask(mask_leaf_root, *leaf_to_root.shape[1:])
    mask_mr = own_mask(mask_mid_root, *mid_to_root.shape[1:])
    pair = lambda a, tile, s: [
        (a, (1, tile, a.shape[2]), lambda i, l=l: (2 * s + l, i, 0), 2 * PIECE * l, a.shape[2]) for l in (0, 1)
    ]
    one = lambda a, tile, s: [(a, (1, tile, a.shape[2]), lambda i: (s, i, 0), 0, a.shape[2])]

    streams = (0, 1)
    first = [spread(lax.dynamic_index_in_dim(right_leaf, 2 * s + k, 0, False)) for s in streams]
    leaf_half, leaf_pieces = [], []
    for s in streams:
        part = apply(first[s], pair(inverse_leaf, 128, s), 256, 128, separate=True, leafwise=True)
        mine, other = halve(part)
        leaf_half.append(mine + other)
    leaf_pieces = [spread(h) for h in leaf_half]
    solved_leaf = [both_halves(h) for h in leaf_half]

    mid_half = []
    for s in streams:
        part = apply(
            leaf_pieces[s], pair(leaf_to_mid, 256, s), 512, 256, mask=mask_lm[2 * s : 2 * s + 2], leafwise=True
        )
        mine, other = halve(part.reshape(2, PIECE, n))
        right = lax.dynamic_index_in_dim(right_mid[s].reshape(2, PIECE, n), k, 0, False)
        mid_half.append(right - (mine + other))
    root_part, resid_pieces = None, []
    for s in streams:

        def make(mine, s=s, before=root_part):
            p = leaf_pieces[s]
            return apply(
                (gate(p[0], mine),) + p[1:],
                [(t[0],) + t[1:] for t in pair(leaf_to_root, 256, s)],
                1024,
                256,
                mask=mask_lr[2 * s : 2 * s + 2],
                add=before,
                leafwise=True,
            )

        pieces, root_part = spread(mid_half[s], make)
        resid_pieces.append(pieces)

    solved_half = []
    for s in streams:
        part = apply(resid_pieces[s], one(inverse_mid, 256, s), 512, 256)
        mine, other = halve(part.reshape(2, PIECE, n))
        solved_half.append(mine + other)
    mid_pieces = [spread(h) for h in solved_half]
    solved_mid = [both_halves(h) for h in solved_half]

    root_part = apply(
        mid_pieces[0], one(mid_to_root[0:1], 256, 0), 1024, 256, mask=mask_mr[0:1], add=root_part
    )
    root_half = []
    for g in (0, 1):
        part = apply(
            mid_pieces[1],
            one(mid_to_root[1:2], 256, 0),
            512,
            256,
            first_tile=2 * g,
            mask=mask_mr[1:2, 4 * g : 4 * g + 4],
            add=root_part,
        )
        mine, other = halve(part.reshape(2, PIECE, n))
        right = lax.dynamic_index_in_dim(right_root.reshape(4, PIECE, n), 2 * g + k, 0, False)
        root_half.append(right - (mine + other))
    root_pieces = [spread(h) for h in root_half]

    columns = lambda g: [
        (inverse_root, (256, 512), lambda i, b=b: (i, 2 * b + g), 2 * PIECE * b, 2 * PIECE) for b in (0, 1)
    ]
    part = apply(root_pieces[0], columns(0), 1024, 256)
    mine, theirs = [], []
    for g in (0, 1):
        final = apply(root_pieces[1], columns(1), 512, 256, first_tile=2 * g, add=part)
        one_half, other = halve(final.reshape(2, PIECE, n))
        mine.append(one_half + other)
        theirs.append(send(mine[g], TO_CORE))
    first_group = lax.broadcasted_iota(jnp.int32, (2, 2, 1, 1), 0) == 0
    here = lax.broadcasted_iota(jnp.int32, (2, 2, 1, 1), 1) == k
    solved_root = jnp.where(
        here, jnp.where(first_group, mine[0], mine[1]), jnp.where(first_group, theirs[0], theirs[1])
    ).reshape(4 * PIECE, n)
    return (
        jnp.concatenate(solved_leaf, axis=0),
        jnp.stack([h.reshape(2 * PIECE, n) for h in solved_mid]),
        solved_root,
    )


def body(*args):
    if lax.axis_size("rows") == 8 and lax.axis_size("cols") == 4 and args[0].shape == (4, PIECE, TILE):
        return grid_body(*args)
    return general_body(*args)


def solution(mesh):
    placed = (
        P(None, "rows", None),
        P(None, "rows", None),
        P("rows", None),
        P(None, "rows", "cols"),
        P(None, "rows", "cols"),
        P("rows", "cols"),
        P(None, "rows", "cols"),
        P(None, "rows", "cols"),
        P(None, "rows", "cols"),
        P(),
        P(),
        P(),
    )
    return jax.shard_map(
        body,
        mesh=mesh,
        in_specs=placed,
        out_specs=(P(None, "rows", None), P(None, "rows", None), P("rows", None)),
        check_vma=False,
    )
```

```python
import functools

import jax
import jax.numpy as jnp
from jax import lax
from jax.experimental import pallas as pl
from jax.experimental.pallas import tpu as pltpu
from jax.sharding import PartitionSpec as P

TILE = 128
AXES = ("rows", "cols")
BF16 = jnp.bfloat16
F32 = jnp.float32


def product(matrix, vector):
    return jnp.einsum(
        "src,sck->srk",
        matrix,
        vector,
        precision=lax.Precision.HIGHEST,
        preferred_element_type=jnp.float32,
    )


def masked(values, pattern):
    rows_dev = values.shape[1]
    cols_dev = values.shape[2]
    row_ids = lax.axis_index("rows") * rows_dev + lax.iota(jnp.int32, rows_dev)
    col_ids = lax.axis_index("cols") * cols_dev + lax.iota(jnp.int32, cols_dev)
    row_hot = (row_ids[:, None] // TILE == lax.iota(jnp.int32, pattern.shape[1])[None, :]).astype(F32)
    col_hot = (col_ids[:, None] // TILE == lax.iota(jnp.int32, pattern.shape[2])[None, :]).astype(F32)
    return values * jnp.einsum("ra,sab,cb->src", row_hot, pattern.astype(F32), col_hot)


def fetch_columns(block):
    gathered = lax.all_gather(block, "rows", axis=1, tiled=True)
    col_width = gathered.shape[1] // lax.axis_size("cols")
    return lax.dynamic_slice_in_dim(gathered, lax.axis_index("cols") * col_width, col_width, 1)


def general_body(
    right_leaf,
    right_mid,
    right_root,
    inverse_leaf,
    inverse_mid,
    inverse_root,
    leaf_to_mid,
    leaf_to_root,
    mid_to_root,
    mask_leaf_mid,
    mask_leaf_root,
    mask_mid_root,
):
    factor_lm = masked(leaf_to_mid, mask_leaf_mid)
    factor_lr = masked(leaf_to_root, mask_leaf_root)
    factor_mr = masked(mid_to_root, mask_mid_root)
    solved_leaf = lax.psum(product(inverse_leaf, fetch_columns(right_leaf)), "cols")
    leaf_columns = fetch_columns(solved_leaf)
    terms = product(factor_lm, leaf_columns)
    mid_part = terms.reshape(2, 2, terms.shape[1], terms.shape[2]).sum(axis=1)
    resid_mid = right_mid - lax.psum(mid_part, "cols")
    solved_mid = lax.psum(product(inverse_mid, fetch_columns(resid_mid)), "cols")
    mid_columns = fetch_columns(solved_mid)
    root_part = product(factor_lr, leaf_columns).sum(axis=0) + product(factor_mr, mid_columns).sum(axis=0)
    resid_root = right_root - lax.psum(root_part, "cols")
    solved_root = lax.psum(product(inverse_root[None], fetch_columns(resid_root[None])), "cols")
    return (solved_leaf, solved_mid, solved_root[0])


PIECE = 256


def flat(x, y, z, k):
    return (2 * z + y) * 4 + 2 * x + k


PLACES = [(x, y, z, k) for x in (0, 1) for y in (0, 1) for z in range(4) for k in (0, 1)]
TO_CORE = [(flat(x, y, z, k), flat(x, y, z, 1 - k)) for x, y, z, k in PLACES]
TO_X = [(flat(x, y, z, k), flat(1 - x, y, z, k)) for x, y, z, k in PLACES]
TO_Y = [(flat(x, y, z, k), flat(x, 1 - y, z, k)) for x, y, z, k in PLACES]
TO_Z = [(flat(x, y, z, k), flat(x, y, z ^ 1, k)) for x, y, z, k in PLACES]
TO_YZ = [(flat(x, y, z, k), flat(x, 1 - y, z ^ 1, k)) for x, y, z, k in PLACES]
TO_FAR = [(flat(x, y, z, k), flat(x, y, 3 - z, k)) for x, y, z, k in PLACES if z // 2 == x]


def send(value, pairs):
    return lax.ppermute(value, AXES, pairs)


def place():
    r, c = lax.axis_index("rows"), lax.axis_index("cols")
    return c // 2, r % 2, r // 2, c % 2


def halve(part):
    k = place()[3]
    other = send(part, TO_CORE)
    mine = lax.dynamic_index_in_dim(part, k, 0, False) + lax.dynamic_index_in_dim(other, k, 0, False)
    return mine, send(mine, TO_X)


def both_halves(mine):
    k = place()[3]
    other = send(mine, TO_CORE)
    first = k == 0
    return jnp.stack([jnp.where(first, mine, other), jnp.where(first, other, mine)])


def gate(value, after):
    return lax.optimization_barrier((value, after))[0]


def spread(mine, make=None):
    x, y, z, k = place()
    far = send(mine, TO_FAR)
    own = jnp.where(z // 2 == x, mine, far)
    made = None
    if make is not None:
        made = make(mine)
        own = gate(own, made)
    beside, above, across = send(own, TO_Y), send(own, TO_Z), send(own, TO_YZ)
    same = jnp.where(z // 2 == x, z % 2, 1 - z % 2) == k
    swapped = send(jnp.stack([jnp.where(same, above, own), jnp.where(same, across, beside)]), TO_CORE)
    pieces = (own, beside, above, across, swapped)
    return pieces if make is None else (pieces, made)


def split(value):
    high = value.astype(BF16)
    return high, (value - high.astype(F32)).astype(BF16)


def kernel_body(spans, has_mask, has_add, separate, leafwise, groups, *refs):
    sets, refs = refs[: 5 * groups], refs[5 * groups :]
    count = len(spans)
    mats, refs = refs[:count], refs[count:]
    if has_mask:
        mask, refs = refs[0], refs[1:]
    if has_add:
        add, refs = refs[0], refs[1:]
    out, held = refs
    step = pl.program_id(0)
    n = out.shape[-1]

    @pl.when(step == 0)
    def _():
        r, c = lax.axis_index("rows"), lax.axis_index("cols")
        y, k = lax.rem(r, 2), lax.rem(c, 2)
        z = r // 2
        same = jnp.where(z // 2 == c // 2, lax.rem(z, 2), 1 - lax.rem(z, 2)) == k

        for s in range(groups):
            own, beside, above, across, swapped = sets[5 * s : 5 * s + 5]

            def put(value, y_of, half, s=s):
                row = half * (2 * PIECE) + y_of * PIECE if leafwise else y_of * (2 * PIECE) + half * PIECE
                row = pl.multiple_of(row + s * (4 * PIECE), PIECE)
                high, low = split(value)
                held[pl.ds(row, PIECE), :n] = high
                held[pl.ds(row, PIECE), n:] = low

            @pl.when(same)
            def _():
                put(own[...], y, k)
                put(beside[...], 1 - y, k)

            @pl.when(jnp.logical_not(same))
            def _():
                put(above[...], y, k)
                put(across[...], 1 - y, k)

            put(swapped[0], y, 1 - k)
            put(swapped[1], 1 - y, 1 - k)

    total = None
    for t, (start, width) in enumerate(spans):
        leaf = t if len(mats) == 1 or mats[t].ndim == 3 else 0
        a = mats[t][0] if mats[t].ndim == 3 else mats[t][...]
        if has_mask:
            rows = a.shape[0] // TILE
            a = jnp.concatenate(
                [a[q * TILE : (q + 1) * TILE] * mask[t, pl.ds(step * rows + q, 1), :] for q in range(rows)], axis=0
            )
        high, low = split(a)
        x = held[start : start + width, :]
        wide = jnp.dot(high, x, preferred_element_type=F32)
        value = jnp.dot(low, x[:, :n], preferred_element_type=F32) + wide[:, n:] + wide[:, :n]
        if separate:
            out[t] = value
        else:
            total = value if total is None else total + value
    if not separate:
        if has_add:
            total = total + add[...]
        out[...] = total


def apply(pieces, terms, rows, row_tile, first_tile=0, mask=None, add=None, separate=False, leafwise=False):
    n = pieces[0].shape[-1]
    steps = rows // row_tile
    full = lambda a: pl.BlockSpec(a.shape, lambda i, d=a.ndim: (0,) * d)
    operands = list(pieces)
    specs = [full(a) for a in pieces]
    for array, block, index, _, _ in terms:
        operands.append(array)
        specs.append(pl.BlockSpec(block, lambda i, index=index: index(i + first_tile)))
    if mask is not None:
        operands.append(mask)
        specs.append(full(mask))
    if add is not None:
        operands.append(add)
        specs.append(pl.BlockSpec((row_tile, n), lambda i: (i + first_tile, 0)))
    if separate:
        shape = (len(terms), rows, n)
        out_spec = pl.BlockSpec((len(terms), row_tile, n), lambda i: (0, i, 0))
    else:
        shape = (rows, n)
        out_spec = pl.BlockSpec((row_tile, n), lambda i: (i, 0))
    work = sum(rows * t[4] for t in terms)
    return pl.pallas_call(
        functools.partial(
            kernel_body, tuple((t[3], t[4]) for t in terms), mask is not None, add is not None, separate, leafwise, len(pieces) // 5
        ),
        out_shape=jax.ShapeDtypeStruct(shape, F32),
        grid_spec=pltpu.PrefetchScalarGridSpec(
            num_scalar_prefetch=0,
            grid=(steps,),
            in_specs=specs,
            out_specs=out_spec,
            scratch_shapes=[pltpu.VMEM((len(pieces) // 5 * 4 * PIECE, 2 * n), BF16)],
        ),
        compiler_params=pltpu.CompilerParams(vmem_limit_bytes=32 << 20),
        cost_estimate=pl.CostEstimate(flops=8 * work * n, bytes_accessed=4 * work, transcendentals=0),
    )(*operands)


def own_mask(pattern, rows, cols):
    r, c = lax.axis_index("rows"), lax.axis_index("cols")
    tr, tc = rows // TILE, cols // TILE
    part = lax.dynamic_slice(pattern, (0, r * tr, c * tc), (pattern.shape[0], tr, tc))
    return jnp.repeat(part.astype(F32), TILE, axis=2)


def grid_body(
    right_leaf,
    right_mid,
    right_root,
    inverse_leaf,
    inverse_mid,
    inverse_root,
    leaf_to_mid,
    leaf_to_root,
    mid_to_root,
    mask_leaf_mid,
    mask_leaf_root,
    mask_mid_root,
):
    k = place()[3]
    n = right_root.shape[-1]
    mask_lm = own_mask(mask_leaf_mid, *leaf_to_mid.shape[1:])
    mask_lr = own_mask(mask_leaf_root, *leaf_to_root.shape[1:])
    mask_mr = own_mask(mask_mid_root, *mid_to_root.shape[1:])
    pair = lambda a, tile, s: [
        (a, (1, tile, a.shape[2]), lambda i, l=l: (2 * s + l, i, 0), 2 * PIECE * l, a.shape[2]) for l in (0, 1)
    ]
    one = lambda a, tile, s: [(a, (1, tile, a.shape[2]), lambda i: (s, i, 0), 0, a.shape[2])]

    streams = (0, 1)
    first = [spread(lax.dynamic_index_in_dim(right_leaf, 2 * s + k, 0, False)) for s in streams]
    leaf_half, leaf_pieces = [], []
    for s in streams:
        part = apply(first[s], pair(inverse_leaf, 128, s), 256, 128, separate=True, leafwise=True)
        mine, other = halve(part)
        leaf_half.append(mine + other)
    leaf_pieces = [spread(h) for h in leaf_half]
    solved_leaf = [both_halves(h) for h in leaf_half]

    mid_half = []
    for s in streams:
        part = apply(
            leaf_pieces[s], pair(leaf_to_mid, 256, s), 512, 256, mask=mask_lm[2 * s : 2 * s + 2], leafwise=True
        )
        mine, other = halve(part.reshape(2, PIECE, n))
        right = lax.dynamic_index_in_dim(right_mid[s].reshape(2, PIECE, n), k, 0, False)
        mid_half.append(right - (mine + other))
    root_part, resid_pieces = None, []
    for s in streams:

        def make(mine, s=s, before=root_part):
            p = leaf_pieces[s]
            return apply(
                (gate(p[0], mine),) + p[1:],
                [(t[0],) + t[1:] for t in pair(leaf_to_root, 256, s)],
                1024,
                256,
                mask=mask_lr[2 * s : 2 * s + 2],
                add=before,
                leafwise=True,
            )

        pieces, root_part = spread(mid_half[s], make)
        resid_pieces.append(pieces)

    solved_half = []
    for s in streams:
        part = apply(resid_pieces[s], one(inverse_mid, 256, s), 512, 256)
        mine, other = halve(part.reshape(2, PIECE, n))
        solved_half.append(mine + other)
    mid_pieces = [spread(h) for h in solved_half]
    solved_mid = [both_halves(h) for h in solved_half]

    root_part = apply(
        mid_pieces[0], one(mid_to_root[0:1], 256, 0), 1024, 256, mask=mask_mr[0:1], add=root_part
    )
    root_half = []
    for g in (0, 1):
        part = apply(
            mid_pieces[1],
            one(mid_to_root[1:2], 256, 0),
            512,
            256,
            first_tile=2 * g,
            mask=mask_mr[1:2, 4 * g : 4 * g + 4],
            add=root_part,
        )
        mine, other = halve(part.reshape(2, PIECE, n))
        right = lax.dynamic_index_in_dim(right_root.reshape(4, PIECE, n), 2 * g + k, 0, False)
        root_half.append(right - (mine + other))
    root_pieces = [spread(h) for h in root_half]

    columns = [
        (inverse_root, (256, 512), lambda i, b=b, s=s: (i, 2 * b + s), 4 * PIECE * s + 2 * PIECE * b, 2 * PIECE)
        for s in (0, 1)
        for b in (0, 1)
    ]
    mine, theirs = [], []
    for g in (0, 1):
        final = apply(root_pieces[0] + root_pieces[1], columns, 512, 256, first_tile=2 * g)
        one_half, other = halve(final.reshape(2, PIECE, n))
        mine.append(one_half + other)
        theirs.append(send(mine[g], TO_CORE))
    first_group = lax.broadcasted_iota(jnp.int32, (2, 2, 1, 1), 0) == 0
    here = lax.broadcasted_iota(jnp.int32, (2, 2, 1, 1), 1) == k
    solved_root = jnp.where(
        here, jnp.where(first_group, mine[0], mine[1]), jnp.where(first_group, theirs[0], theirs[1])
    ).reshape(4 * PIECE, n)
    return (
        jnp.concatenate(solved_leaf, axis=0),
        jnp.stack([h.reshape(2 * PIECE, n) for h in solved_mid]),
        solved_root,
    )


def body(*args):
    if lax.axis_size("rows") == 8 and lax.axis_size("cols") == 4 and args[0].shape == (4, PIECE, TILE):
        return grid_body(*args)
    return general_body(*args)


def solution(mesh):
    placed = (
        P(None, "rows", None),
        P(None, "rows", None),
        P("rows", None),
        P(None, "rows", "cols"),
        P(None, "rows", "cols"),
        P("rows", "cols"),
        P(None, "rows", "cols"),
        P(None, "rows", "cols"),
        P(None, "rows", "cols"),
        P(),
        P(),
        P(),
    )
    return jax.shard_map(
        body,
        mesh=mesh,
        in_specs=placed,
        out_specs=(P(None, "rows", None), P(None, "rows", None), P("rows", None)),
        check_vma=False,
    )
```
